32 devices in a mesh: aa: 4 (over y, x), ta: 8 (over z, core).
Axes of the slice: x: 2, y: 2, z: 4, core: 2. Of those that a mesh axis runs over, the one named last changes fastest.
Arguments:
- voltages: bfloat16 [1024, 49152], P('aa', 'ta'), may hold values from -6 to 6
Outputs:
- visibility: bfloat16 [2, 512, 1024, 1024], P(None, 'aa', 'ta')
The draws below stay inside these ranges and needn't reach their ends.
All inputs are finite; a program needn't handle non-finite values.
Results may differ from the reference program's by a relative error of at most 0.0078.
Values may be sent and summed in bfloat16 or wider, within the bound.
A program may use at most 256 MiB of HBM per device.

```python
import jax
import jax.numpy as jnp
from jax import lax

INPUTS = 1024
FRAME = 2048
CHANNELS = 512
TAPS = 4
SPECTRA = 24
SAMPLES = 49152


def level_of(stream_key, dims, pieces, smallest, high):
    gain = 1.0
    for axis_at, shards_of in pieces:
        draws = jax.random.uniform(jax.random.fold_in(jax.random.fold_in(stream_key, 6), axis_at), (shards_of,), jnp.float32, smallest / len(pieces), high / len(pieces))
        gain = gain * jnp.repeat(jnp.exp(draws), dims[axis_at] // shards_of).reshape((-1,) + (1,) * (len(dims) - 1 - axis_at))
    return gain


def noise(rng, dims, scale, reach, cuts=(), held_as=jnp.bfloat16):
    drawn = jax.random.normal(rng, dims, jnp.float32) * scale
    if len(cuts) > 0:
        drawn = level_of(rng, dims, cuts, -0.22, 0.18) * drawn
    return jnp.clip(drawn, min=-reach, max=reach).astype(held_as)


def setup_inputs(seed: int = 0) -> dict:
    arg_keys = jax.random.split(jax.random.key(seed), 2)
    voltages = noise(arg_keys[0], (INPUTS, SAMPLES), 1.0, 6.0, ((0, 4), (1, 8)))
    return {"voltages": voltages}


def make_window():
    length = TAPS * FRAME
    place = jnp.arange(length, dtype=jnp.float32)
    spread = (place - length / 2 + 0.5) / FRAME
    taper = 0.5 - 0.5 * jnp.cos(2.0 * jnp.pi * (place + 0.5) / length)
    return (jnp.sinc(spread) * taper).reshape(TAPS, FRAME)

def make_table():
    sample = jnp.arange(FRAME, dtype=jnp.int32)[:, None]
    channel = jnp.arange(CHANNELS, dtype=jnp.int32)[None, :]
    phase = (sample * channel % FRAME).astype(jnp.float32) * (2.0 * jnp.pi / FRAME)
    norm = 1.0 / jnp.sqrt(jnp.float32(FRAME))
    return (jnp.concatenate([jnp.cos(phase), -jnp.sin(phase)], axis=1) * norm).astype(jnp.bfloat16)

def correlate_one(block):
    real_part = block[0].astype(jnp.float32)
    imag_part = block[1].astype(jnp.float32)
    hi = lax.Precision.HIGHEST
    real_out = jnp.einsum('si,sj->ij', real_part, real_part, precision=hi) + jnp.einsum('si,sj->ij', imag_part, imag_part, precision=hi)
    imag_out = jnp.einsum('si,sj->ij', imag_part, real_part, precision=hi) - jnp.einsum('si,sj->ij', real_part, imag_part, precision=hi)
    return (jnp.stack([real_out, imag_out], axis=0) * (1.0 / SPECTRA)).astype(jnp.bfloat16)

def reference(voltages):
    window = make_window()
    table = make_table()
    frames = voltages.reshape(INPUTS, SPECTRA, FRAME).astype(jnp.float32)
    padded = jnp.concatenate([jnp.zeros((INPUTS, TAPS - 1, FRAME), jnp.float32), frames], axis=1)
    filtered = jnp.zeros((INPUTS, SPECTRA, FRAME), jnp.float32)
    for k in range(TAPS):
        filtered = filtered + window[k] * padded[:, k:k + SPECTRA, :]
    filtered = filtered.astype(jnp.bfloat16)
    spectra = jnp.dot(filtered.reshape(INPUTS * SPECTRA, FRAME), table, preferred_element_type=jnp.float32).astype(jnp.bfloat16)
    spectra = spectra.reshape(INPUTS, SPECTRA, 2, CHANNELS).transpose(3, 2, 1, 0)
    result = lax.map(correlate_one, spectra)
    return jnp.swapaxes(result, 0, 1)
```

```python
import functools

import jax
import jax.numpy as jnp
import numpy as np
from jax import lax
from jax.experimental import pallas as pl
from jax.experimental.pallas import tpu as pltpu
from jax.sharding import PartitionSpec as P

INPUTS = 1024
FRAME = 2048
CHANNELS = 512
TAPS = 4
LANES = 128


def make_window():
    length = TAPS * FRAME
    place = np.arange(length, dtype=np.float64)
    spread = (place - length / 2 + 0.5) / FRAME
    taper = 0.5 - 0.5 * np.cos(2.0 * np.pi * (place + 0.5) / length)
    return (np.sinc(spread) * taper).reshape(TAPS, FRAME).astype(np.float32)


def make_turns():
    channel = np.arange(CHANNELS)[:, None]

    def turn(step, count):
        phase = (channel * np.arange(count)[None, :] * step % FRAME) * (2.0 * np.pi / FRAME)
        return np.cos(phase), np.sin(phase)

    coarse_cos, coarse_sin = turn(LANES, FRAME // LANES)
    fine_cos, fine_sin = turn(1, LANES)
    norm = 1.0 / np.sqrt(FRAME)
    coarse = np.concatenate([coarse_cos, coarse_sin], axis=1)
    fine = np.concatenate([fine_cos * norm, fine_sin * norm], axis=1)
    return coarse.astype(np.float32), fine.astype(np.float32)


def table_kernel(coarse_ref, fine_ref, out_ref):
    count = FRAME // LANES

    @pl.loop(0, CHANNELS // 16)
    def _(step):
        at = pl.multiple_of(step * 16, 16)
        here = pl.ds(at, 16)
        fine_cos, fine_sin = fine_ref[here, :LANES], fine_ref[here, LANES:]
        for a in range(count):
            columns = slice(a * LANES, (a + 1) * LANES)
            coarse_cos = coarse_ref[here, a : a + 1]
            coarse_sin = coarse_ref[here, count + a : count + a + 1]
            real = coarse_cos * fine_cos - coarse_sin * fine_sin
            imag = -(coarse_sin * fine_cos + coarse_cos * fine_sin)
            out_ref[0, here, columns] = real.astype(jnp.bfloat16)
            out_ref[1, here, columns] = imag.astype(jnp.bfloat16)


def make_table():
    coarse, fine = make_turns()
    return pl.pallas_call(
        table_kernel,
        out_shape=jax.ShapeDtypeStruct((2, CHANNELS, FRAME), jnp.bfloat16),
        compiler_params=pltpu.CompilerParams(vmem_limit_bytes=16 * 2**20),
        cost_estimate=pl.CostEstimate(
            flops=2**23, bytes_accessed=2**23, transcendentals=0
        ),
    )(jnp.asarray(coarse), jnp.asarray(fine))


def dft_kernel(core_ref, *refs, pick, count, unread):
    window_ref, table_ref = refs[-4 - unread : -2 - unread]
    blocks, (out_ref, filtered_ref) = refs[: -4 - unread], refs[-2:]
    inputs = blocks[0].shape[0]
    rows = min(16, inputs)

    def filter_from(earlier, current):
        def frame(at, index):
            ref, place = (earlier, index) if index < count else (current, index - count)
            return ref[pl.ds(at, rows), place * FRAME : (place + 1) * FRAME].astype(jnp.float32)

        @pl.loop(0, inputs // rows)
        def _(step):
            at = pl.multiple_of(step * rows, rows)
            for s in range(count):
                total = window_ref[0:1, :] * frame(at, s + count - TAPS + 1)
                for k in range(1, TAPS):
                    total = total + window_ref[k : k + 1, :] * frame(at, s + k + count - TAPS + 1)
                filtered_ref[s, pl.ds(at, rows), :] = total.astype(jnp.bfloat16)

    @pl.when((pl.program_id(0) == 0) & (pl.program_id(1) == 0))
    def _():
        for core, (earlier, current) in enumerate(pick):
            pl.when(core_ref[0] == core)(
                functools.partial(filter_from, blocks[earlier], blocks[current])
            )

    for s in range(count):
        out_ref[0, 0, s] = lax.dot_general(
            table_ref[0],
            filtered_ref[s],
            (((1,), (1,)), ((), ())),
            preferred_element_type=jnp.float32,
        ).astype(jnp.bfloat16)


def dft(core, blocks, pick, window, table, n_aa, count, after=()):
    inputs = blocks[0].shape[0]
    chan_dev = CHANNELS // n_aa
    whole = lambda q, p, core_ref: (0, 0)
    flops = 2 * count * inputs * FRAME * 2 * CHANNELS
    return pl.pallas_call(
        functools.partial(dft_kernel, pick=pick, count=count, unread=len(after)),
        grid_spec=pltpu.PrefetchScalarGridSpec(
            num_scalar_prefetch=1,
            grid=(n_aa, 2),
            in_specs=[pl.BlockSpec(block.shape, whole) for block in blocks]
            + [
                pl.BlockSpec((TAPS, FRAME), whole),
                pl.BlockSpec((1, chan_dev, FRAME), lambda q, p, core_ref: (p, q, 0)),
            ]
            + [pl.BlockSpec(memory_space=pl.ANY)] * len(after),
            out_specs=pl.BlockSpec(
                (1, 1, count, chan_dev, inputs), lambda q, p, core_ref: (q, p, 0, 0, 0)
            ),
            scratch_shapes=[pltpu.VMEM((count, inputs, FRAME), jnp.bfloat16)],
        ),
        out_shape=jax.ShapeDtypeStruct((n_aa, 2, count, chan_dev, inputs), jnp.bfloat16),
        compiler_params=pltpu.CompilerParams(vmem_limit_bytes=40 * 2**20),
        cost_estimate=pl.CostEstimate(
            flops=flops, bytes_accessed=len(blocks) * blocks[0].size * 2 + 2**22, transcendentals=0
        ),
    )(core, *blocks, window, table, *after)


def correlate_kernel(core_ref, first_ref, second_ref, spread_ref, *refs, scale, groups):
    out_ref, columns_ref = refs[-2:]
    halves, chans, depth, lanes = first_ref.shape
    full = halves * depth
    size = columns_ref.shape[0]
    if full < size:
        columns_ref[full:, :] = jnp.zeros((size - full, 2 * lanes), jnp.bfloat16)
    own = pl.ds(pl.multiple_of(core_ref[0] * lanes, lanes), lanes)
    group_of = lax.rem(lax.broadcasted_iota(jnp.int32, (1, size), 1), depth) // (depth // groups)
    masks = [
        jnp.where(group_of == group, 1.0, 0.0).astype(jnp.bfloat16) for group in range(groups)
    ]

    @pl.loop(0, chans)
    def _(c):
        for at, ref in enumerate((first_ref, second_ref)):
            for block in range(halves // 2):
                place = (at * (halves // 2) + block) * depth
                for core in range(2):
                    columns_ref[place : place + depth, core * lanes : (core + 1) * lanes] = ref[
                        2 * block + core, c
                    ]
        columns = columns_ref[...]
        left = lax.dot_general(
            columns_ref[:, own],
            spread_ref[...],
            (((0,), (0,)), ((), ())),
            preferred_element_type=jnp.float32,
        ).astype(jnp.bfloat16)
        for p in range(2):
            part = left[:, p * size : (p + 1) * size]
            for group in range(groups):
                total = jnp.dot(
                    part * masks[group], columns, preferred_element_type=jnp.float32
                )
                out_ref[p, c, :, group * 2 * lanes : (group + 1) * 2 * lanes] = (
                    total * scale
                ).astype(jnp.bfloat16)


def spread_rows(group, halves, depth, groups):
    part = depth // groups
    full, size = halves * depth, 256
    row = lax.broadcasted_iota(jnp.int32, (size, 2 * size), 0)
    column = lax.broadcasted_iota(jnp.int32, (size, 2 * size), 1)
    turned, column = column // size, column % size
    same = (row // depth == column // depth) & (row < full) & (column < full)
    same = same & (row % depth // part == group)
    row, column = row % part, column % part
    count = part // 2
    straight = jnp.where(row == column, 1.0, 0.0)
    swap = jnp.where(row == column + count, 1.0, 0.0) - jnp.where(row + count == column, 1.0, 0.0)
    values = jnp.where(turned == 1, swap, straight)
    return jnp.where(same, values, 0.0).astype(jnp.bfloat16)


def correlate(core, first, second, spread, result, at, chan_dev, n_aa, scale):
    halves, chans, depth, lanes = second.shape
    step = min(8, chans)
    start = at // step
    out_shape = jax.ShapeDtypeStruct((2, chan_dev, lanes, INPUTS), jnp.bfloat16)
    extra = [] if result is None else [result]
    return pl.pallas_call(
        functools.partial(correlate_kernel, scale=scale, groups=n_aa),
        grid_spec=pltpu.PrefetchScalarGridSpec(
            num_scalar_prefetch=1,
            grid=(chans // step,),
            in_specs=[
                pl.BlockSpec((halves, step, depth, lanes), lambda c, core_ref: (0, start + c, 0, 0)),
                pl.BlockSpec((halves, step, depth, lanes), lambda c, core_ref: (0, c, 0, 0)),
                pl.BlockSpec(spread.shape, lambda c, core_ref: (0, 0)),
            ]
            + [pl.BlockSpec(memory_space=pl.ANY)] * len(extra),
            out_specs=pl.BlockSpec(
                (2, step, lanes, INPUTS), lambda c, core_ref: (0, start + c, 0, 0)
            ),
            scratch_shapes=[pltpu.VMEM((256, 2 * lanes), jnp.bfloat16)],
        ),
        out_shape=out_shape,
        input_output_aliases={4: 0} if extra else {},
        compiler_params=pltpu.CompilerParams(vmem_limit_bytes=60 * 2**20),
        cost_estimate=pl.CostEstimate(
            flops=4 * chans * lanes * INPUTS * 256,
            bytes_accessed=chans * (4 * lanes * INPUTS + 4 * halves * depth * lanes),
            transcendentals=0,
        ),
    )(core, first, second, spread, *extra)


def shifted(value, axis, steps):
    count = lax.axis_size(axis)
    leading, last = (max(0, -steps), min(count, count - steps))
    return lax.ppermute(value, axis, [(source, source + steps) for source in range(leading, last)])


def plain_window():
    length = TAPS * FRAME
    place = jnp.arange(length, dtype=jnp.float32)
    spread = (place - length / 2 + 0.5) / FRAME
    taper = 0.5 - 0.5 * jnp.cos(2.0 * jnp.pi * (place + 0.5) / length)
    return (jnp.sinc(spread) * taper).reshape(TAPS, FRAME)


def plain_table():
    sample = jnp.arange(FRAME, dtype=jnp.int32)[:, None]
    column = jnp.arange(2 * CHANNELS, dtype=jnp.int32)[None, :]
    channel = column % CHANNELS
    phase = (sample * channel % FRAME).astype(jnp.float32) * (2.0 * jnp.pi / FRAME)
    norm = 1.0 / jnp.sqrt(jnp.float32(FRAME))
    values = jnp.where(column < CHANNELS, jnp.cos(phase), -jnp.sin(phase))
    return (values * norm).astype(jnp.bfloat16)


def left_operand(rows):
    first = jnp.concatenate([rows[0], rows[1]], axis=2)
    second = jnp.concatenate([rows[1], -rows[0]], axis=2)
    return jnp.stack([first, second], axis=0)


def plain_correlate(left, columns):
    return jnp.einsum("pcsi,pcsj->cij", left, columns, preferred_element_type=jnp.float32)


def finish(merged, row_count, scale):
    chan_dev = merged.shape[0]
    shaped = merged.reshape(chan_dev, 2, row_count, merged.shape[2])
    return (jnp.swapaxes(shaped, 0, 1) * scale).astype(jnp.bfloat16)


def plain_per_device(voltages):
    in_dev = voltages.shape[0]
    spec_dev = voltages.shape[1] // FRAME
    n_ta = lax.axis_size("ta")
    frames = voltages.reshape(in_dev, spec_dev, FRAME)
    earlier = shifted(frames, "ta", 1)
    padded = jnp.concatenate([earlier, frames], axis=1)
    window = plain_window()
    filtered = jnp.zeros((in_dev, spec_dev, FRAME), jnp.float32)
    for k in range(TAPS):
        filtered = filtered + window[k] * padded[:, k : k + spec_dev, :].astype(jnp.float32)
    filtered = filtered.astype(jnp.bfloat16)
    table = plain_table()
    spectra = jnp.einsum("isn,nk->ksi", filtered, table, preferred_element_type=jnp.float32).astype(
        jnp.bfloat16
    )
    spectra = spectra.reshape(2, CHANNELS, spec_dev, in_dev)
    row_count = INPUTS // n_ta
    scale = 1.0 / (spec_dev * n_ta)
    own_rows = lax.all_to_all(
        lax.all_to_all(spectra, "aa", split_axis=1, concat_axis=3, tiled=True),
        "ta",
        split_axis=3,
        concat_axis=2,
        tiled=True,
    )
    left = left_operand(own_rows)
    merged = plain_correlate(left, lax.all_gather(own_rows, "ta", axis=3, tiled=True))
    return finish(merged, row_count, scale)


def pack_kernel(spectra_ref, unread_ref, *out_refs):
    at = 0
    for out_ref in out_refs:
        out_ref[...] = spectra_ref[at : at + out_ref.shape[0]]
        at += out_ref.shape[0]


def pack(spectra, after, sizes):
    return pl.pallas_call(
        pack_kernel,
        in_specs=[
            pl.BlockSpec(memory_space=pltpu.VMEM),
            pl.BlockSpec(memory_space=pl.ANY),
        ],
        out_shape=[
            jax.ShapeDtypeStruct((size,) + spectra.shape[1:], spectra.dtype) for size in sizes
        ],
        compiler_params=pltpu.CompilerParams(vmem_limit_bytes=60 * 2**20),
        cost_estimate=pl.CostEstimate(
            flops=0, bytes_accessed=4 * spectra.size, transcendentals=0
        ),
    )(spectra, after)


def chunks_of(chan_dev):
    part = chan_dev // 8
    sizes = [3 * part, 3 * part, 2 * part]
    return [(sum(sizes[:at]), size) for at, size in enumerate(sizes)]


def per_device(voltages):
    in_dev = voltages.shape[0]
    count = voltages.shape[1] // FRAME
    n_ta, n_aa = lax.axis_size("ta"), lax.axis_size("aa")
    half = in_dev // 2
    chan_dev = CHANNELS // n_aa
    fits = in_dev == 2 * LANES and INPUTS == n_ta * LANES and 2 * count * n_ta * n_aa <= 256
    if not fits or count < TAPS - 1 or chan_dev % 64:
        return plain_per_device(voltages)
    scale = 1.0 / (count * n_ta)
    me = lax.axis_index("ta")
    core = lax.rem(me, 2)

    odd = range(1, n_ta, 2)
    halo_even = lax.ppermute(voltages[:half], "ta", [(d, d + 1) for d in odd if d + 1 < n_ta])
    halo_odd = lax.ppermute(voltages[half:], "ta", [(d, d + 2) for d in odd if d + 2 < n_ta])
    keep = lax.dynamic_slice_in_dim(voltages, core * half, half, 0)
    give = lax.dynamic_slice_in_dim(voltages, (1 - core) * half, half, 0)
    got = lax.ppermute(give, "ta", [(d, d ^ 1) for d in range(n_ta)])

    window = jnp.asarray(make_window())
    table = make_table()
    where = core.astype(jnp.int32).reshape(1)

    def exchange(spectra):
        moved = lax.all_to_all(spectra, "aa", split_axis=0, concat_axis=0, tiled=True)
        return moved.transpose(3, 0, 1, 2, 4).reshape(chan_dev, n_aa * 2 * count, half)

    def gather(parts):
        return lax.all_gather(parts, "ta", axis=0)

    late = exchange(dft(where, [keep, got], ((0, 1), (1, 0)), window, table, n_aa, count))
    first = gather(late)
    early = exchange(
        dft(
            where,
            [keep, got, halo_even, halo_odd],
            ((2, 0), (3, 1)),
            window,
            table,
            n_aa,
            count,
            after=[late],
        )
    )
    spread = spread_rows(me // 2, n_ta, n_aa * 2 * count, n_aa)
    result = None
    chunks = chunks_of(chan_dev)
    packed = pack(early, first, [size for _, size in chunks])
    for (at, size), part in zip(chunks, packed):
        second = gather(part)
        result = correlate(where, first, second, spread, result, at, chan_dev, n_aa, scale)
    return result


def solution(mesh):
    in_specs = (P("aa", "ta"),)
    out_specs = P(None, "aa", "ta", None)
    return jax.shard_map(
        per_device, mesh=mesh, in_specs=in_specs, out_specs=out_specs, check_vma=False
    )
```

```python
import functools

import jax
import jax.numpy as jnp
import numpy as np
from jax import lax
from jax.experimental import pallas as pl
from jax.experimental.pallas import tpu as pltpu
from jax.sharding import PartitionSpec as P

INPUTS = 1024
FRAME = 2048
CHANNELS = 512
TAPS = 4
LANES = 128


def make_window():
    length = TAPS * FRAME
    place = np.arange(length, dtype=np.float64)
    spread = (place - length / 2 + 0.5) / FRAME
    taper = 0.5 - 0.5 * np.cos(2.0 * np.pi * (place + 0.5) / length)
    return (np.sinc(spread) * taper).reshape(TAPS, FRAME).astype(np.float32)


def make_turns():
    channel = np.arange(CHANNELS)[:, None]

    def turn(step, count):
        phase = (channel * np.arange(count)[None, :] * step % FRAME) * (2.0 * np.pi / FRAME)
        return np.cos(phase), np.sin(phase)

    coarse_cos, coarse_sin = turn(LANES, FRAME // LANES)
    fine_cos, fine_sin = turn(1, LANES)
    norm = 1.0 / np.sqrt(FRAME)
    coarse = np.concatenate([coarse_cos, coarse_sin], axis=1)
    fine = np.concatenate([fine_cos * norm, fine_sin * norm], axis=1)
    return coarse.astype(np.float32), fine.astype(np.float32)


def table_kernel(coarse_ref, fine_ref, out_ref):
    count = FRAME // LANES

    @pl.loop(0, CHANNELS // 16)
    def _(step):
        at = pl.multiple_of(step * 16, 16)
        here = pl.ds(at, 16)
        fine_cos, fine_sin = fine_ref[here, :LANES], fine_ref[here, LANES:]
        for a in range(count):
            columns = slice(a * LANES, (a + 1) * LANES)
            coarse_cos = coarse_ref[here, a : a + 1]
            coarse_sin = coarse_ref[here, count + a : count + a + 1]
            real = coarse_cos * fine_cos - coarse_sin * fine_sin
            imag = -(coarse_sin * fine_cos + coarse_cos * fine_sin)
            out_ref[0, here, columns] = real.astype(jnp.bfloat16)
            out_ref[1, here, columns] = imag.astype(jnp.bfloat16)


def make_table():
    coarse, fine = make_turns()
    return pl.pallas_call(
        table_kernel,
        out_shape=jax.ShapeDtypeStruct((2, CHANNELS, FRAME), jnp.bfloat16),
        compiler_params=pltpu.CompilerParams(vmem_limit_bytes=16 * 2**20),
        cost_estimate=pl.CostEstimate(
            flops=2**23, bytes_accessed=2**23, transcendentals=0
        ),
    )(jnp.asarray(coarse), jnp.asarray(fine))


def dft_kernel(core_ref, *refs, pick, count, unread):
    window_ref, table_ref = refs[-4 - unread : -2 - unread]
    blocks, (out_ref, filtered_ref) = refs[: -4 - unread], refs[-2:]
    inputs = blocks[0].shape[0]
    rows = min(16, inputs)

    def filter_from(earlier, current):
        def frame(at, index):
            ref, place = (earlier, index) if index < count else (current, index - count)
            return ref[pl.ds(at, rows), place * FRAME : (place + 1) * FRAME].astype(jnp.float32)

        @pl.loop(0, inputs // rows)
        def _(step):
            at = pl.multiple_of(step * rows, rows)
            for s in range(count):
                total = window_ref[0:1, :] * frame(at, s + count - TAPS + 1)
                for k in range(1, TAPS):
                    total = total + window_ref[k : k + 1, :] * frame(at, s + k + count - TAPS + 1)
                filtered_ref[s, pl.ds(at, rows), :] = total.astype(jnp.bfloat16)

    @pl.when((pl.program_id(0) == 0) & (pl.program_id(1) == 0))
    def _():
        for core, (earlier, current) in enumerate(pick):
            pl.when(core_ref[0] == core)(
                functools.partial(filter_from, blocks[earlier], blocks[current])
            )

    for s in range(count):
        out_ref[0, 0, s] = lax.dot_general(
            table_ref[0],
            filtered_ref[s],
            (((1,), (1,)), ((), ())),
            preferred_element_type=jnp.float32,
        ).astype(jnp.bfloat16)


def dft(core, blocks, pick, window, table, n_aa, count, after=()):
    inputs = blocks[0].shape[0]
    chan_dev = CHANNELS // n_aa
    whole = lambda q, p, core_ref: (0, 0)
    flops = 2 * count * inputs * FRAME * 2 * CHANNELS
    return pl.pallas_call(
        functools.partial(dft_kernel, pick=pick, count=count, unread=len(after)),
        grid_spec=pltpu.PrefetchScalarGridSpec(
            num_scalar_prefetch=1,
            grid=(n_aa, 2),
            in_specs=[pl.BlockSpec(block.shape, whole) for block in blocks]
            + [
                pl.BlockSpec((TAPS, FRAME), whole),
                pl.BlockSpec((1, chan_dev, FRAME), lambda q, p, core_ref: (p, q, 0)),
            ]
            + [pl.BlockSpec(memory_space=pl.ANY)] * len(after),
            out_specs=pl.BlockSpec(
                (1, 1, count, chan_dev, inputs), lambda q, p, core_ref: (q, p, 0, 0, 0)
            ),
            scratch_shapes=[pltpu.VMEM((count, inputs, FRAME), jnp.bfloat16)],
        ),
        out_shape=jax.ShapeDtypeStruct((n_aa, 2, count, chan_dev, inputs), jnp.bfloat16),
        compiler_params=pltpu.CompilerParams(vmem_limit_bytes=40 * 2**20),
        cost_estimate=pl.CostEstimate(
            flops=flops, bytes_accessed=len(blocks) * blocks[0].size * 2 + 2**22, transcendentals=0
        ),
    )(core, *blocks, window, table, *after)


def correlate_kernel(core_ref, first_ref, second_ref, spread_ref, *refs, scale, groups):
    out_ref, columns_ref, left_ref = refs[-3:]
    halves, chans, depth, lanes = first_ref.shape
    full = halves * depth
    size = columns_ref.shape[0]
    if full < size:
        columns_ref[full:, :] = jnp.zeros((size - full, 2 * lanes), jnp.bfloat16)
    own = pl.ds(pl.multiple_of(core_ref[0] * lanes, lanes), lanes)
    group_of = lax.rem(lax.broadcasted_iota(jnp.int32, (1, size), 1), depth) // (depth // groups)
    masks = [
        jnp.where(group_of == group, 1.0, 0.0).astype(jnp.bfloat16) for group in range(groups)
    ]

    @pl.loop(0, chans)
    def _(c):
        for at, ref in enumerate((first_ref, second_ref)):
            for block in range(halves // 2):
                place = (at * (halves // 2) + block) * depth
                for core in range(2):
                    columns_ref[place : place + depth, core * lanes : (core + 1) * lanes] = ref[
                        2 * block + core, c
                    ]
        left = lax.dot_general(
            columns_ref[:, own],
            spread_ref[...],
            (((0,), (0,)), ((), ())),
            preferred_element_type=jnp.float32,
        ).astype(jnp.bfloat16)
        for p in range(2):
            part = left[:, p * size : (p + 1) * size]
            for group in range(groups):
                place = (p * groups + group) * lanes
                left_ref[place : place + lanes, :] = part * masks[group]
        total = jnp.dot(left_ref[...], columns_ref[...], preferred_element_type=jnp.float32)
        value = (total * scale).astype(jnp.bfloat16)
        for p in range(2):
            for group in range(groups):
                place = (p * groups + group) * lanes
                out_ref[p, c, :, group * 2 * lanes : (group + 1) * 2 * lanes] = value[
                    place : place + lanes
                ]


def spread_rows(group, halves, depth, groups):
    part = depth // groups
    full, size = halves * depth, 256
    row = lax.broadcasted_iota(jnp.int32, (size, 2 * size), 0)
    column = lax.broadcasted_iota(jnp.int32, (size, 2 * size), 1)
    turned, column = column // size, column % size
    same = (row // depth == column // depth) & (row < full) & (column < full)
    same = same & (row % depth // part == group)
    row, column = row % part, column % part
    count = part // 2
    straight = jnp.where(row == column, 1.0, 0.0)
    swap = jnp.where(row == column + count, 1.0, 0.0) - jnp.where(row + count == column, 1.0, 0.0)
    values = jnp.where(turned == 1, swap, straight)
    return jnp.where(same, values, 0.0).astype(jnp.bfloat16)


def correlate(core, first, second, spread, result, at, chan_dev, n_aa, scale):
    halves, chans, depth, lanes = second.shape
    step = min(8, chans)
    start = at // step
    out_shape = jax.ShapeDtypeStruct((2, chan_dev, lanes, INPUTS), jnp.bfloat16)
    extra = [] if result is None else [result]
    return pl.pallas_call(
        functools.partial(correlate_kernel, scale=scale, groups=n_aa),
        grid_spec=pltpu.PrefetchScalarGridSpec(
            num_scalar_prefetch=1,
            grid=(chans // step,),
            in_specs=[
                pl.BlockSpec((halves, step, depth, lanes), lambda c, core_ref: (0, start + c, 0, 0)),
                pl.BlockSpec((halves, step, depth, lanes), lambda c, core_ref: (0, c, 0, 0)),
                pl.BlockSpec(spread.shape, lambda c, core_ref: (0, 0)),
            ]
            + [pl.BlockSpec(memory_space=pl.ANY)] * len(extra),
            out_specs=pl.BlockSpec(
                (2, step, lanes, INPUTS), lambda c, core_ref: (0, start + c, 0, 0)
            ),
            scratch_shapes=[
                pltpu.VMEM((256, 2 * lanes), jnp.bfloat16),
                pltpu.VMEM((2 * n_aa * lanes, 256), jnp.bfloat16),
            ],
        ),
        out_shape=out_shape,
        input_output_aliases={4: 0} if extra else {},
        compiler_params=pltpu.CompilerParams(vmem_limit_bytes=60 * 2**20),
        cost_estimate=pl.CostEstimate(
            flops=4 * chans * lanes * INPUTS * 256,
            bytes_accessed=chans * (4 * lanes * INPUTS + 4 * halves * depth * lanes),
            transcendentals=0,
        ),
    )(core, first, second, spread, *extra)


def shifted(value, axis, steps):
    count = lax.axis_size(axis)
    leading, last = (max(0, -steps), min(count, count - steps))
    return lax.ppermute(value, axis, [(source, source + steps) for source in range(leading, last)])


def plain_window():
    length = TAPS * FRAME
    place = jnp.arange(length, dtype=jnp.float32)
    spread = (place - length / 2 + 0.5) / FRAME
    taper = 0.5 - 0.5 * jnp.cos(2.0 * jnp.pi * (place + 0.5) / length)
    return (jnp.sinc(spread) * taper).reshape(TAPS, FRAME)


def plain_table():
    sample = jnp.arange(FRAME, dtype=jnp.int32)[:, None]
    column = jnp.arange(2 * CHANNELS, dtype=jnp.int32)[None, :]
    channel = column % CHANNELS
    phase = (sample * channel % FRAME).astype(jnp.float32) * (2.0 * jnp.pi / FRAME)
    norm = 1.0 / jnp.sqrt(jnp.float32(FRAME))
    values = jnp.where(column < CHANNELS, jnp.cos(phase), -jnp.sin(phase))
    return (values * norm).astype(jnp.bfloat16)


def left_operand(rows):
    first = jnp.concatenate([rows[0], rows[1]], axis=2)
    second = jnp.concatenate([rows[1], -rows[0]], axis=2)
    return jnp.stack([first, second], axis=0)


def plain_correlate(left, columns):
    return jnp.einsum("pcsi,pcsj->cij", left, columns, preferred_element_type=jnp.float32)


def finish(merged, row_count, scale):
    chan_dev = merged.shape[0]
    shaped = merged.reshape(chan_dev, 2, row_count, merged.shape[2])
    return (jnp.swapaxes(shaped, 0, 1) * scale).astype(jnp.bfloat16)


def plain_per_device(voltages):
    in_dev = voltages.shape[0]
    spec_dev = voltages.shape[1] // FRAME
    n_ta = lax.axis_size("ta")
    frames = voltages.reshape(in_dev, spec_dev, FRAME)
    earlier = shifted(frames, "ta", 1)
    padded = jnp.concatenate([earlier, frames], axis=1)
    window = plain_window()
    filtered = jnp.zeros((in_dev, spec_dev, FRAME), jnp.float32)
    for k in range(TAPS):
        filtered = filtered + window[k] * padded[:, k : k + spec_dev, :].astype(jnp.float32)
    filtered = filtered.astype(jnp.bfloat16)
    table = plain_table()
    spectra = jnp.einsum("isn,nk->ksi", filtered, table, preferred_element_type=jnp.float32).astype(
        jnp.bfloat16
    )
    spectra = spectra.reshape(2, CHANNELS, spec_dev, in_dev)
    row_count = INPUTS // n_ta
    scale = 1.0 / (spec_dev * n_ta)
    own_rows = lax.all_to_all(
        lax.all_to_all(spectra, "aa", split_axis=1, concat_axis=3, tiled=True),
        "ta",
        split_axis=3,
        concat_axis=2,
        tiled=True,
    )
    left = left_operand(own_rows)
    merged = plain_correlate(left, lax.all_gather(own_rows, "ta", axis=3, tiled=True))
    return finish(merged, row_count, scale)


def pack_kernel(spectra_ref, *refs, unread):
    out_refs = refs[unread:]
    at = 0
    for out_ref in out_refs:
        out_ref[...] = spectra_ref[at : at + out_ref.shape[0]]
        at += out_ref.shape[0]


def pack(spectra, after, sizes):
    return pl.pallas_call(
        functools.partial(pack_kernel, unread=len(after)),
        in_specs=[pl.BlockSpec(memory_space=pltpu.VMEM)]
        + [pl.BlockSpec(memory_space=pl.ANY)] * len(after),
        out_shape=[
            jax.ShapeDtypeStruct((size,) + spectra.shape[1:], spectra.dtype) for size in sizes
        ],
        compiler_params=pltpu.CompilerParams(vmem_limit_bytes=60 * 2**20),
        cost_estimate=pl.CostEstimate(
            flops=0, bytes_accessed=4 * spectra.size, transcendentals=0
        ),
    )(spectra, *after)


def chunks_of(chan_dev):
    part = chan_dev // 8
    sizes = [5 * part, 3 * part]
    return [(sum(sizes[:at]), size) for at, size in enumerate(sizes)]


def per_device(voltages):
    in_dev = voltages.shape[0]
    count = voltages.shape[1] // FRAME
    n_ta, n_aa = lax.axis_size("ta"), lax.axis_size("aa")
    half = in_dev // 2
    chan_dev = CHANNELS // n_aa
    fits = in_dev == 2 * LANES and INPUTS == n_ta * LANES and 2 * count * n_ta * n_aa <= 256
    if not fits or count < TAPS - 1 or chan_dev % 64:
        return plain_per_device(voltages)
    scale = 1.0 / (count * n_ta)
    me = lax.axis_index("ta")
    core = lax.rem(me, 2)

    odd = range(1, n_ta, 2)
    halo_even = lax.ppermute(voltages[:half], "ta", [(d, d + 1) for d in odd if d + 1 < n_ta])
    halo_odd = lax.ppermute(voltages[half:], "ta", [(d, d + 2) for d in odd if d + 2 < n_ta])
    keep = lax.dynamic_slice_in_dim(voltages, core * half, half, 0)
    give = lax.dynamic_slice_in_dim(voltages, (1 - core) * half, half, 0)
    got = lax.ppermute(give, "ta", [(d, d ^ 1) for d in range(n_ta)])

    window = jnp.asarray(make_window())
    table = make_table()
    where = core.astype(jnp.int32).reshape(1)

    def exchange(spectra):
        moved = lax.all_to_all(spectra, "aa", split_axis=0, concat_axis=0, tiled=True)
        return moved.transpose(3, 0, 1, 2, 4).reshape(chan_dev, n_aa * 2 * count, half)

    def gather(parts):
        return lax.all_gather(parts, "ta", axis=0)

    late = exchange(dft(where, [keep, got], ((0, 1), (1, 0)), window, table, n_aa, count))
    (late,) = pack(late, [halo_even, halo_odd], [chan_dev])
    first = gather(late)
    early = exchange(
        dft(
            where,
            [keep, got, halo_even, halo_odd],
            ((2, 0), (3, 1)),
            window,
            table,
            n_aa,
            count,
            after=[late],
        )
    )
    spread = spread_rows(me // 2, n_ta, n_aa * 2 * count, n_aa)
    result = None
    chunks = chunks_of(chan_dev)
    packed = pack(early, [first], [size for _, size in chunks])
    for (at, size), part in zip(chunks, packed):
        second = gather(part)
        result = correlate(where, first, second, spread, result, at, chan_dev, n_aa, scale)
    return result


def solution(mesh):
    in_specs = (P("aa", "ta"),)
    out_specs = P(None, "aa", "ta", None)
    return jax.shard_map(
        per_device, mesh=mesh, in_specs=in_specs, out_specs=out_specs, check_vma=False
    )
```
